32 devices in a mesh: ctx: 16 (over z, x, core), head: 2 (over y).
Axes of the slice: x: 2, y: 2, z: 4, core: 2. Of those that a mesh axis runs over, the one named last changes fastest.
Arguments:
- queries: bfloat16 [64, 2048], P(('ctx', 'head')), may hold values from -150 to 150
- new_block_keys: bfloat16 [64, 512], P(('ctx', 'head')), may hold values from -6 to 6
- new_block_values: bfloat16 [64, 512], P(('ctx', 'head')), may hold values from -6 to 6
- stored_keys: bfloat16 [7168, 512], P('ctx', 'head'), may hold values from -6 to 6
- stored_values: bfloat16 [7168, 512], P('ctx', 'head'), may hold values from -6 to 6
- stretch_start: int32 [1], replicated, may hold values from 3584 to 7168
- block_order: int32 [32], replicated, may hold values from 0 to 31, each once
Outputs:
- attended: bfloat16 [64, 2048], P(('ctx', 'head'))
The draws below stay inside these ranges and needn't reach their ends.
Inputs may be any that keep to these rules, and one draw needn't show every extreme that they name: `block_order`: each value appears once.
All inputs are finite; a program needn't handle non-finite values.
Results may differ from the reference program's by a relative error of at most 0.0049.
Values may be sent and summed in bfloat16 or wider, within the bound.
A program may use at most 128 MiB of HBM per device.

```python
import math
import jax
import jax.numpy as jnp
from jax import lax

QUERY_HEADS = 16
KEY_VALUE_HEADS = 4
HEAD_WIDTH = 128
Q_CTX = 4
BLOCK_TOKENS = 64
CACHED_SLOTS = 7168
N_CTX = 16


def cache_base(key):
    unscaled_scores = jax.random.normal(jax.random.fold_in(key, 7001), (CACHED_SLOTS, KEY_VALUE_HEADS * HEAD_WIDTH), jnp.float32)
    return jnp.clip(unscaled_scores, -6.0, 6.0)


def draw_stored_keys(key, part):
    base = cache_base(key)
    return base.astype(jnp.bfloat16)


def draw_queries(key, part):
    unscaled_scores = jax.random.normal(jax.random.fold_in(key, 7002), (BLOCK_TOKENS, QUERY_HEADS * HEAD_WIDTH), jnp.float32)
    base = jnp.clip(unscaled_scores, -6.0, 6.0)
    return base.astype(jnp.bfloat16)


def steps_of(stream_key, dims, shards, least, top_value):
    level = 1.0
    for position, shards_of in shards:
        heights = jax.random.uniform(jax.random.fold_in(jax.random.fold_in(stream_key, 6), position), (shards_of,), jnp.float32, least / len(shards), top_value / len(shards))
        level = level * jnp.repeat(jnp.exp(heights), dims[position] // shards_of).reshape((-1,) + (1,) * (len(dims) - 1 - position))
    return level


def centred(rng, shape, deviation, limit, pieces=(), kind=jnp.bfloat16):
    level = steps_of(rng, shape, pieces, -0.22, 0.18) if pieces else 1.0
    result = jax.random.normal(rng, shape, jnp.float32) * deviation * level
    return jnp.minimum(jnp.maximum(result, -limit), limit).astype(kind)


def setup_inputs(seed: int = 0) -> dict:
    splits = jax.random.split(jax.random.key(seed), 8)
    return {
        "queries": draw_queries(jax.random.fold_in(splits[7], 71), 0),
        "new_block_keys": centred(splits[1], (BLOCK_TOKENS, KEY_VALUE_HEADS * HEAD_WIDTH), 1.0, 6.0, ((0, 32),)),
        "new_block_values": centred(splits[2], (BLOCK_TOKENS, KEY_VALUE_HEADS * HEAD_WIDTH), 1.0, 6.0, ((0, 32),)),
        "stored_keys": draw_stored_keys(jax.random.fold_in(splits[7], 71), 0),
        "stored_values": centred(splits[4], (CACHED_SLOTS, KEY_VALUE_HEADS * HEAD_WIDTH), 1.0, 6.0, ((0, 16), (1, 2))),
        "stretch_start": jax.random.randint(splits[5], (1,), CACHED_SLOTS // 2, CACHED_SLOTS + 1).astype(jnp.int32),
        "block_order": jax.random.permutation(splits[6], 2 * N_CTX).astype(jnp.int32),
    }


NEG_FILL = -1e+30

def reference(queries, new_block_keys, new_block_values, stored_keys, stored_values, stretch_start, block_order):
    half_rows = Q_CTX // 2
    stretch_first = stretch_start[0]
    row_ids = jnp.arange(BLOCK_TOKENS, dtype=jnp.int32)
    query_pos = stretch_first + block_order[row_ids // half_rows] * half_rows + row_ids % half_rows
    cache_pos = jnp.arange(CACHED_SLOTS, dtype=jnp.int32)
    key_pos = jnp.concatenate([cache_pos, query_pos])
    usable = jnp.concatenate([cache_pos < stretch_first, jnp.ones((BLOCK_TOKENS,), dtype=bool)])
    query_group_width = QUERY_HEADS // KEY_VALUE_HEADS
    every_row = CACHED_SLOTS + BLOCK_TOKENS
    joined_keys = jnp.concatenate([stored_keys, new_block_keys], 0).astype(jnp.float32).reshape(every_row, KEY_VALUE_HEADS, HEAD_WIDTH)
    joined_values = jnp.concatenate([stored_values, new_block_values], 0).astype(jnp.float32).reshape(every_row, KEY_VALUE_HEADS, HEAD_WIDTH)
    score_scale = 1.0 / math.sqrt(HEAD_WIDTH)
    rows_of_block = math.gcd(BLOCK_TOKENS, 64)

    def one_block(block_index):
        start_row = block_index * rows_of_block
        query_row_block = lax.dynamic_slice_in_dim(queries, start_row, rows_of_block, 0).astype(jnp.float32)
        query_row_block = query_row_block.reshape(rows_of_block, KEY_VALUE_HEADS, query_group_width, HEAD_WIDTH)
        pos_q = lax.dynamic_slice_in_dim(query_pos, start_row, rows_of_block, 0)
        scores = jnp.einsum('bhgd,khd->bhgk', query_row_block, joined_keys) * score_scale
        allowed = usable[None, :] & (key_pos[None, :] <= pos_q[:, None])
        allowed = allowed[:, None, None, :]
        row_peak = lax.optimization_barrier(jnp.max(jnp.where(allowed, scores, NEG_FILL), axis=-1, keepdims=True))
        weights = jnp.where(allowed, jnp.exp(scores - row_peak), 0.0)
        totals = lax.optimization_barrier(jnp.sum(weights, axis=-1))
        rounded = lax.optimization_barrier(weights.astype(jnp.bfloat16)).astype(jnp.float32)
        mixed = jnp.einsum('bhgk,khd->bhgd', rounded, joined_values) / totals[..., None]
        return mixed.reshape(rows_of_block, QUERY_HEADS * HEAD_WIDTH).astype(jnp.bfloat16)
    blocks_out = lax.map(one_block, jnp.arange(BLOCK_TOKENS // rows_of_block, dtype=jnp.int32))
    return blocks_out.reshape(BLOCK_TOKENS, QUERY_HEADS * HEAD_WIDTH)
```

```python
import functools
import math

import jax
import jax.numpy as jnp
from jax import lax
from jax.experimental import pallas as pl
from jax.experimental.pallas import tpu as pltpu
from jax.sharding import PartitionSpec as P

QUERY_HEADS = 16
KEY_VALUE_HEADS = 4
HEAD_WIDTH = 128
NEG_FILL = -1e30
FAR = 2**30
TILE = 16
STAT_ROWS = 2
MESH = pl.DeviceIdType.MESH
F32 = jnp.float32
BF16 = jnp.bfloat16


def each(first, count, body):
    if count - first <= 64:
        for step in range(first, count):
            body(step)
    else:
        lax.fori_loop(first, count, lambda step, _: body(step), None)


def kernel(
    n_ctx,
    n_head,
    stretch_ref,
    order_ref,
    q_ref,
    nk_ref,
    nv_ref,
    k_hbm,
    v_hbm,
    out_ref,
    qsend,
    qrecv,
    kbuf,
    vbuf,
    fresh,
    osend,
    orecv,
    local_sem,
    q_sems,
    kv_send,
    kv_recv,
    o_sems,
):
    n = n_ctx * n_head
    rows = q_ref.shape[0]
    cache = k_hbm.shape[0]
    width = k_hbm.shape[1]
    kv_heads = width // HEAD_WIDTH
    heads = QUERY_HEADS // n_head
    lines = heads * rows
    half = rows * n_head // 2
    per_half = half // rows
    ctx = lax.axis_index("ctx")
    head = lax.axis_index("head")
    me = ctx * n_head + head

    def place(slot):
        return (slot // n_head, lax.rem(slot, n_head))

    load_k = pltpu.make_async_copy(k_hbm, kbuf.at[pl.ds(0, cache)], local_sem.at[0])
    load_v = pltpu.make_async_copy(v_hbm, vbuf.at[pl.ds(0, cache)], local_sem.at[1])
    load_k.start()
    load_v.start()

    barrier = pltpu.get_barrier_semaphore()

    def greet(step):
        pl.semaphore_signal(
            barrier, inc=1, device_id=place(lax.rem(me + step, n)), device_id_type=MESH
        )

    each(1, n, greet)

    block = q_ref[...].astype(F32)
    for h in range(n_head):
        pieces = [
            block[:, (h * heads + i) * HEAD_WIDTH : (h * heads + i + 1) * HEAD_WIDTH]
            for i in range(heads)
        ]
        qsend[h] = jnp.concatenate(pieces, axis=0).astype(BF16)
    blank = jnp.zeros((TILE - rows, width), F32)
    for t, ref in enumerate((nk_ref, nv_ref)):
        new = ref[...].astype(F32)
        for h in range(n_head):
            part = new[:, h * width : (h + 1) * width]
            fresh[h, t] = jnp.concatenate([part, blank], axis=0).astype(BF16)

    pl.semaphore_wait(barrier, n - 1)

    spot = pl.ds(pl.multiple_of(cache + TILE * head, TILE), TILE)
    swaps = []
    for step in range(1, n_head):
        to = lax.rem(head + step, n_head)
        for t, buf in enumerate((kbuf, vbuf)):
            swap = pltpu.make_async_remote_copy(
                src_ref=fresh.at[to, t],
                dst_ref=buf.at[spot],
                send_sem=kv_send.at[step - 1, t],
                recv_sem=kv_recv.at[step - 1, t],
                device_id=(ctx, to),
                device_id_type=MESH,
            )
            swap.start()
            swaps.append(swap)

    def send_queries(step):
        to_ctx, to_head = place(lax.rem(me + step, n))
        pltpu.make_async_remote_copy(
            src_ref=qsend.at[to_head],
            dst_ref=qrecv.at[me],
            send_sem=q_sems.at[0],
            recv_sem=q_sems.at[1],
            device_id=(to_ctx, to_head),
            device_id_type=MESH,
        ).start()

    each(1, n, send_queries)
    qrecv[me] = qsend[head]
    kbuf[spot] = fresh[head, 0]
    vbuf[spot] = fresh[head, 1]

    def start_of(slot):
        return order_ref[slot // per_half] * half + lax.rem(slot, per_half) * rows

    total_keys = cache + TILE * n_head
    split = (cache // 128) * 128
    column = lax.broadcasted_iota(jnp.int32, (1, total_keys), 1)
    key_pos = jnp.where(column + ctx * cache < stretch_ref[0], -1, FAR)
    for h in range(n_head):
        offset = column - (cache + TILE * h)
        pos = jnp.where(offset < rows, start_of(ctx * n_head + h) + offset, FAR)
        key_pos = jnp.where(offset >= 0, pos, key_pos)

    load_k.wait()
    load_v.wait()
    for swap in swaps:
        swap.wait()
    q_all = qrecv.at[pl.ds(0, n - 1)]
    q_done = pltpu.make_async_remote_copy(
        src_ref=q_all,
        dst_ref=q_all,
        send_sem=q_sems.at[0],
        recv_sem=q_sems.at[1],
        device_id=(ctx, head),
        device_id_type=MESH,
    )
    q_done.wait_recv()

    group = min(n, 32)
    size = group * lines
    scale = 1.0 / math.sqrt(HEAD_WIDTH)

    def attend(index):
        first = index * group
        line = lax.broadcasted_iota(jnp.int32, (size, HEAD_WIDTH), 0)
        line = lax.rem(line, lines)
        kv_of = line // (lines // kv_heads)
        q = qrecv[pl.ds(first, group)].astype(F32).reshape(size, HEAD_WIDTH)
        q = jnp.concatenate(
            [jnp.where(kv_of == g, q, 0.0) for g in range(kv_heads)], axis=1
        ).astype(BF16)
        scores = (
            lax.dot_general(
                q, kbuf[...], (((1,), (1,)), ((), ())), preferred_element_type=F32
            )
            * scale
        )
        tail = total_keys - split
        query_pos = jnp.concatenate(
            [jnp.full((lines, tail), start_of(first + i), jnp.int32) for i in range(group)],
            axis=0,
        )
        query_pos = query_pos + lax.rem(
            lax.broadcasted_iota(jnp.int32, (size, tail), 0), rows
        )
        old = jnp.where(key_pos[:, :split] < 0, scores[:, :split], NEG_FILL)
        new = jnp.where(key_pos[:, split:] <= query_pos, scores[:, split:], NEG_FILL)
        scores = jnp.concatenate([old, new], axis=1)
        peak = jnp.max(scores, axis=1, keepdims=True)
        weights = jnp.exp(scores - peak)
        total = jnp.sum(weights, axis=1, keepdims=True)
        sums = lax.dot_general(
            weights.astype(BF16),
            vbuf[...],
            (((1,), (0,)), ((), ())),
            preferred_element_type=F32,
        )
        part = sums[:, :HEAD_WIDTH]
        for g in range(1, kv_heads):
            part = jnp.where(kv_of == g, sums[:, g * HEAD_WIDTH : (g + 1) * HEAD_WIDTH], part)
        part = part / total
        mass = peak + jnp.log(total)
        high = mass.astype(BF16).astype(F32)
        rest = mass - high
        mid = rest.astype(BF16).astype(F32)
        low = rest - mid
        lane = lax.broadcasted_iota(jnp.int32, (size, HEAD_WIDTH), 1)
        stat = jnp.where(lane < lines, high, jnp.where(lane < 2 * lines, mid, low))
        stat = jnp.where((lane < 3 * lines) & (lax.rem(lane, lines) == line), stat, 0.0)
        stat = jnp.sum(stat.reshape(group, lines, HEAD_WIDTH), axis=1, keepdims=True)
        osend[pl.ds(first, group), 0:lines] = part.reshape(group, lines, HEAD_WIDTH).astype(BF16)
        osend[pl.ds(first, group), lines : lines + STAT_ROWS] = jnp.broadcast_to(
            stat, (group, STAT_ROWS, HEAD_WIDTH)
        ).astype(BF16)

    each(0, n // group, attend)

    def send_parts(step):
        slot = lax.rem(me + step, n)
        pltpu.make_async_remote_copy(
            src_ref=osend.at[slot],
            dst_ref=orecv.at[me],
            send_sem=o_sems.at[0],
            recv_sem=o_sems.at[1],
            device_id=place(slot),
            device_id_type=MESH,
        ).start()

    each(1, n, send_parts)
    orecv[me] = osend[me]
    q_done.wait_send()
    o_all = orecv.at[pl.ds(0, n - 1)]
    o_done = pltpu.make_async_remote_copy(
        src_ref=o_all,
        dst_ref=o_all,
        send_sem=o_sems.at[0],
        recv_sem=o_sems.at[1],
        device_id=(ctx, head),
        device_id_type=MESH,
    )
    o_done.wait_recv()

    lane = lax.broadcasted_iota(jnp.int32, (lines, HEAD_WIDTH), 1)
    line = lax.broadcasted_iota(jnp.int32, (lines, HEAD_WIDTH), 0)
    mine = (lane < 3 * lines) & (lax.rem(lane, lines) == line)
    parts = orecv[:, 0:lines].astype(F32).reshape(n_ctx, n_head, lines, HEAD_WIDTH)
    stats = orecv[:, lines : lines + STAT_ROWS].astype(F32)
    stats = stats.reshape(n_ctx, n_head, STAT_ROWS, HEAD_WIDTH)
    for h in range(n_head):
        spread = jnp.where(mine[None], stats[:, h, 0:1], 0.0)
        mass = jnp.sum(spread, axis=2, keepdims=True)
        top = jnp.max(mass, axis=0, keepdims=True)
        share = jnp.exp(mass - top)
        result = jnp.sum(share * parts[:, h], axis=0) / jnp.sum(share, axis=0)
        for i in range(heads):
            at = (h * heads + i) * HEAD_WIDTH
            out_ref[:, at : at + HEAD_WIDTH] = result[i * rows : (i + 1) * rows].astype(BF16)
    o_done.wait_send()


def on_device(
    n_ctx,
    n_head,
    queries,
    new_block_keys,
    new_block_values,
    stored_keys,
    stored_values,
    stretch_start,
    block_order,
):
    n = n_ctx * n_head
    rows = queries.shape[0]
    cache, width = stored_keys.shape
    lines = QUERY_HEADS // n_head * rows
    total_keys = cache + TILE * n_head
    dma = pltpu.SemaphoreType.DMA
    return pl.pallas_call(
        functools.partial(kernel, n_ctx, n_head),
        out_shape=jax.ShapeDtypeStruct(queries.shape, BF16),
        in_specs=[pl.BlockSpec(memory_space=pltpu.SMEM)] * 2
        + [pl.BlockSpec(memory_space=pltpu.VMEM)] * 3
        + [pl.BlockSpec(memory_space=pl.ANY)] * 2,
        out_specs=pl.BlockSpec(memory_space=pltpu.VMEM),
        scratch_shapes=[
            pltpu.VMEM((n_head, lines, HEAD_WIDTH), BF16),
            pltpu.VMEM((n, lines, HEAD_WIDTH), BF16),
            pltpu.VMEM((total_keys, width), BF16),
            pltpu.VMEM((total_keys, width), BF16),
            pltpu.VMEM((n_head, 2, TILE, width), BF16),
            pltpu.VMEM((n, lines + STAT_ROWS, HEAD_WIDTH), BF16),
            pltpu.VMEM((n, lines + STAT_ROWS, HEAD_WIDTH), BF16),
            dma((2,)),
            dma((2,)),
            dma((n_head - 1, 2)),
            dma((n_head - 1, 2)),
            dma((2,)),
        ],
        compiler_params=pltpu.CompilerParams(
            collective_id=0, has_side_effects=True, vmem_limit_bytes=48 * 1024 * 1024
        ),
    )(
        stretch_start,
        block_order,
        queries,
        new_block_keys,
        new_block_values,
        stored_keys,
        stored_values,
    )


def solution(mesh):
    return jax.shard_map(
        functools.partial(on_device, mesh.shape["ctx"], mesh.shape["head"]),
        mesh=mesh,
        in_specs=(
            P(("ctx", "head"), None),
            P(("ctx", "head"), None),
            P(("ctx", "head"), None),
            P("ctx", "head"),
            P("ctx", "head"),
            P(),
            P(),
        ),
        out_specs=P(("ctx", "head"), None),
        check_vma=False,
    )
```

```python
import functools
import math

import jax
import jax.numpy as jnp
from jax import lax
from jax.experimental import pallas as pl
from jax.experimental.pallas import tpu as pltpu
from jax.sharding import PartitionSpec as P

QUERY_HEADS = 16
KEY_VALUE_HEADS = 4
HEAD_WIDTH = 128
NEG_FILL = -1e30
FAR = 2**30
TILE = 16
STAT_ROWS = 2
MESH = pl.DeviceIdType.MESH
F32 = jnp.float32
BF16 = jnp.bfloat16


def each(first, count, body):
    if count - first <= 64:
        for step in range(first, count):
            body(step)
    else:
        lax.fori_loop(first, count, lambda step, _: body(step), None)


def kernel(
    n_ctx,
    n_head,
    stretch_hbm,
    order_hbm,
    q_hbm,
    nk_hbm,
    nv_hbm,
    k_hbm,
    v_hbm,
    out_ref,
    stretch_ref,
    order_ref,
    q_ref,
    nk_ref,
    nv_ref,
    qsend,
    qrecv,
    kbuf,
    vbuf,
    fresh,
    osend,
    orecv,
    local_sem,
    q_sems,
    kv_send,
    kv_recv,
    o_sems,
):
    n = n_ctx * n_head
    rows = q_hbm.shape[0]
    cache = k_hbm.shape[0]
    width = k_hbm.shape[1]
    kv_heads = width // HEAD_WIDTH
    heads = QUERY_HEADS // n_head
    lines = heads * rows
    half = rows * n_head // 2
    per_half = half // rows
    ctx = lax.axis_index("ctx")
    head = lax.axis_index("head")
    me = ctx * n_head + head

    def place(slot):
        return (slot // n_head, lax.rem(slot, n_head))

    loads = [
        pltpu.make_async_copy(source, target, local_sem.at[i])
        for i, (source, target) in enumerate(
            (
                (q_hbm, q_ref),
                (nk_hbm, nk_ref),
                (nv_hbm, nv_ref),
                (stretch_hbm, stretch_ref),
                (order_hbm, order_ref),
                (k_hbm, kbuf.at[pl.ds(0, cache)]),
                (v_hbm, vbuf.at[pl.ds(0, cache)]),
            )
        )
    ]
    for load in loads:
        load.start()

    barrier = pltpu.get_barrier_semaphore()

    def greet(step):
        pl.semaphore_signal(
            barrier, inc=1, device_id=place(lax.rem(me + step, n)), device_id_type=MESH
        )

    each(1, n, greet)

    for load in loads[:3]:
        load.wait()
    block = q_ref[...].astype(F32)
    for h in range(n_head):
        pieces = [
            block[:, (h * heads + i) * HEAD_WIDTH : (h * heads + i + 1) * HEAD_WIDTH]
            for i in range(heads)
        ]
        qsend[h] = jnp.concatenate(pieces, axis=0).astype(BF16)
    blank = jnp.zeros((TILE - rows, width), F32)
    for t, ref in enumerate((nk_ref, nv_ref)):
        new = ref[...].astype(F32)
        for h in range(n_head):
            part = new[:, h * width : (h + 1) * width]
            fresh[h, t] = jnp.concatenate([part, blank], axis=0).astype(BF16)

    pl.semaphore_wait(barrier, n - 1)

    spot = pl.ds(pl.multiple_of(cache + TILE * head, TILE), TILE)
    swaps = []
    for step in range(1, n_head):
        to = lax.rem(head + step, n_head)
        for t, buf in enumerate((kbuf, vbuf)):
            swap = pltpu.make_async_remote_copy(
                src_ref=fresh.at[to, t],
                dst_ref=buf.at[spot],
                send_sem=kv_send.at[step - 1, t],
                recv_sem=kv_recv.at[step - 1, t],
                device_id=(ctx, to),
                device_id_type=MESH,
            )
            swap.start()
            swaps.append(swap)

    def send_queries(step):
        to_ctx, to_head = place(lax.rem(me + step, n))
        pltpu.make_async_remote_copy(
            src_ref=qsend.at[to_head],
            dst_ref=qrecv.at[me],
            send_sem=q_sems.at[0],
            recv_sem=q_sems.at[1],
            device_id=(to_ctx, to_head),
            device_id_type=MESH,
        ).start()

    each(1, n, send_queries)
    qrecv[me] = qsend[head]
    kbuf[spot] = fresh[head, 0]
    vbuf[spot] = fresh[head, 1]

    for load in loads[3:]:
        load.wait()

    def start_of(slot):
        return order_ref[slot // per_half] * half + lax.rem(slot, per_half) * rows

    total_keys = cache + TILE * n_head
    split = (cache // 128) * 128
    column = lax.broadcasted_iota(jnp.int32, (1, total_keys), 1)
    key_pos = jnp.where(column + ctx * cache < stretch_ref[0], -1, FAR)
    for h in range(n_head):
        offset = column - (cache + TILE * h)
        pos = jnp.where(offset < rows, start_of(ctx * n_head + h) + offset, FAR)
        key_pos = jnp.where(offset >= 0, pos, key_pos)

    for swap in swaps:
        swap.wait()
    q_all = qrecv.at[pl.ds(0, n - 1)]
    q_done = pltpu.make_async_remote_copy(
        src_ref=q_all,
        dst_ref=q_all,
        send_sem=q_sems.at[0],
        recv_sem=q_sems.at[1],
        device_id=(ctx, head),
        device_id_type=MESH,
    )
    q_done.wait_recv()

    group = min(n, 32)
    size = group * lines
    scale = 1.0 / math.sqrt(HEAD_WIDTH)

    def attend(index):
        first = index * group
        line = lax.broadcasted_iota(jnp.int32, (size, HEAD_WIDTH), 0)
        line = lax.rem(line, lines)
        kv_of = line // (lines // kv_heads)
        q = qrecv[pl.ds(first, group)].astype(F32).reshape(size, HEAD_WIDTH)
        q = jnp.concatenate(
            [jnp.where(kv_of == g, q, 0.0) for g in range(kv_heads)], axis=1
        ).astype(BF16)
        scores = (
            lax.dot_general(
                q, kbuf[...], (((1,), (1,)), ((), ())), preferred_element_type=F32
            )
            * scale
        )
        tail = total_keys - split
        query_pos = jnp.concatenate(
            [jnp.full((lines, tail), start_of(first + i), jnp.int32) for i in range(group)],
            axis=0,
        )
        query_pos = query_pos + lax.rem(
            lax.broadcasted_iota(jnp.int32, (size, tail), 0), rows
        )
        old = jnp.where(key_pos[:, :split] < 0, scores[:, :split], NEG_FILL)
        new = jnp.where(key_pos[:, split:] <= query_pos, scores[:, split:], NEG_FILL)
        scores = jnp.concatenate([old, new], axis=1)
        peak = jnp.max(scores, axis=1, keepdims=True)
        weights = jnp.exp(scores - peak)
        total = jnp.sum(weights, axis=1, keepdims=True)
        sums = lax.dot_general(
            weights.astype(BF16),
            vbuf[...],
            (((1,), (0,)), ((), ())),
            preferred_element_type=F32,
        )
        part = sums[:, :HEAD_WIDTH]
        for g in range(1, kv_heads):
            part = jnp.where(kv_of == g, sums[:, g * HEAD_WIDTH : (g + 1) * HEAD_WIDTH], part)
        part = part / total
        mass = peak + jnp.log(total)
        high = mass.astype(BF16).astype(F32)
        rest = mass - high
        mid = rest.astype(BF16).astype(F32)
        low = rest - mid
        lane = lax.broadcasted_iota(jnp.int32, (size, HEAD_WIDTH), 1)
        stat = jnp.where(lane < lines, high, jnp.where(lane < 2 * lines, mid, low))
        stat = jnp.where((lane < 3 * lines) & (lax.rem(lane, lines) == line), stat, 0.0)
        stat = jnp.sum(stat.reshape(group, lines, HEAD_WIDTH), axis=1, keepdims=True)
        osend[pl.ds(first, group), 0:lines] = part.reshape(group, lines, HEAD_WIDTH).astype(BF16)
        osend[pl.ds(first, group), lines : lines + STAT_ROWS] = jnp.broadcast_to(
            stat, (group, STAT_ROWS, HEAD_WIDTH)
        ).astype(BF16)

    each(0, n // group, attend)

    def send_parts(step):
        slot = lax.rem(me + step, n)
        pltpu.make_async_remote_copy(
            src_ref=osend.at[slot],
            dst_ref=orecv.at[me],
            send_sem=o_sems.at[0],
            recv_sem=o_sems.at[1],
            device_id=place(slot),
            device_id_type=MESH,
        ).start()

    each(1, n, send_parts)
    orecv[me] = osend[me]
    q_done.wait_send()
    o_all = orecv.at[pl.ds(0, n - 1)]
    o_done = pltpu.make_async_remote_copy(
        src_ref=o_all,
        dst_ref=o_all,
        send_sem=o_sems.at[0],
        recv_sem=o_sems.at[1],
        device_id=(ctx, head),
        device_id_type=MESH,
    )
    o_done.wait_recv()

    lane = lax.broadcasted_iota(jnp.int32, (lines, HEAD_WIDTH), 1)
    line = lax.broadcasted_iota(jnp.int32, (lines, HEAD_WIDTH), 0)
    mine = (lane < 3 * lines) & (lax.rem(lane, lines) == line)
    parts = orecv[:, 0:lines].astype(F32).reshape(n_ctx, n_head, lines, HEAD_WIDTH)
    stats = orecv[:, lines : lines + STAT_ROWS].astype(F32)
    stats = stats.reshape(n_ctx, n_head, STAT_ROWS, HEAD_WIDTH)
    for h in range(n_head):
        spread = jnp.where(mine[None], stats[:, h, 0:1], 0.0)
        mass = jnp.sum(spread, axis=2, keepdims=True)
        top = jnp.max(mass, axis=0, keepdims=True)
        share = jnp.exp(mass - top)
        result = jnp.sum(share * parts[:, h], axis=0) / jnp.sum(share, axis=0)
        for i in range(heads):
            at = (h * heads + i) * HEAD_WIDTH
            out_ref[:, at : at + HEAD_WIDTH] = result[i * rows : (i + 1) * rows].astype(BF16)
    o_done.wait_send()


def on_device(
    n_ctx,
    n_head,
    queries,
    new_block_keys,
    new_block_values,
    stored_keys,
    stored_values,
    stretch_start,
    block_order,
):
    n = n_ctx * n_head
    rows = queries.shape[0]
    cache, width = stored_keys.shape
    lines = QUERY_HEADS // n_head * rows
    total_keys = cache + TILE * n_head
    dma = pltpu.SemaphoreType.DMA
    return pl.pallas_call(
        functools.partial(kernel, n_ctx, n_head),
        out_shape=jax.ShapeDtypeStruct(queries.shape, BF16),
        in_specs=[pl.BlockSpec(memory_space=pltpu.HBM)] * 7,
        out_specs=pl.BlockSpec(memory_space=pltpu.VMEM),
        scratch_shapes=[
            pltpu.SMEM(stretch_start.shape, jnp.int32),
            pltpu.SMEM(block_order.shape, jnp.int32),
            pltpu.VMEM(queries.shape, BF16),
            pltpu.VMEM(new_block_keys.shape, BF16),
            pltpu.VMEM(new_block_values.shape, BF16),
            pltpu.VMEM((n_head, lines, HEAD_WIDTH), BF16),
            pltpu.VMEM((n, lines, HEAD_WIDTH), BF16),
            pltpu.VMEM((total_keys, width), BF16),
            pltpu.VMEM((total_keys, width), BF16),
            pltpu.VMEM((n_head, 2, TILE, width), BF16),
            pltpu.VMEM((n, lines + STAT_ROWS, HEAD_WIDTH), BF16),
            pltpu.VMEM((n, lines + STAT_ROWS, HEAD_WIDTH), BF16),
            dma((7,)),
            dma((2,)),
            dma((n_head - 1, 2)),
            dma((n_head - 1, 2)),
            dma((2,)),
        ],
        compiler_params=pltpu.CompilerParams(
            collective_id=0, has_side_effects=True, vmem_limit_bytes=48 * 1024 * 1024
        ),
    )(
        stretch_start,
        *[
            pltpu.with_memory_space_constraint(x, pltpu.HBM)
            for x in (
                block_order,
                queries,
                new_block_keys,
                new_block_values,
                stored_keys,
                stored_values,
            )
        ],
    )


def solution(mesh):
    return jax.shard_map(
        functools.partial(on_device, mesh.shape["ctx"], mesh.shape["head"]),
        mesh=mesh,
        in_specs=(
            P(("ctx", "head"), None),
            P(("ctx", "head"), None),
            P(("ctx", "head"), None),
            P("ctx", "head"),
            P("ctx", "head"),
            P(),
            P(),
        ),
        out_specs=P(("ctx", "head"), None),
        check_vma=False,
    )
```

```python
import functools
import math

import jax
import jax.numpy as jnp
from jax import lax
from jax.experimental import pallas as pl
from jax.experimental.pallas import tpu as pltpu
from jax.sharding import PartitionSpec as P

QUERY_HEADS = 16
KEY_VALUE_HEADS = 4
HEAD_WIDTH = 128
NEG_FILL = -1e30
FAR = 2**30
TILE = 16
STAT_ROWS = 2
MESH = pl.DeviceIdType.MESH
F32 = jnp.float32
BF16 = jnp.bfloat16


def each(first, count, body):
    if count - first <= 64:
        for step in range(first, count):
            body(step)
    else:
        lax.fori_loop(first, count, lambda step, _: body(step), None)


def kernel(
    n_ctx,
    n_head,
    stretch_hbm,
    order_hbm,
    q_hbm,
    nk_hbm,
    nv_hbm,
    k_hbm,
    v_hbm,
    out_ref,
    stretch_ref,
    order_ref,
    q_ref,
    nk_ref,
    nv_ref,
    qsend,
    qrecv,
    kbuf,
    vbuf,
    fresh,
    osend,
    orecv,
    local_sem,
    q_sems,
    kv_send,
    kv_recv,
    o_sems,
):
    n = n_ctx * n_head
    rows = q_hbm.shape[0]
    cache = k_hbm.shape[0]
    width = k_hbm.shape[1]
    kv_heads = width // HEAD_WIDTH
    heads = QUERY_HEADS // n_head
    lines = heads * rows
    half = rows * n_head // 2
    per_half = half // rows
    ctx = lax.axis_index("ctx")
    head = lax.axis_index("head")
    me = ctx * n_head + head

    def place(slot):
        return (slot // n_head, lax.rem(slot, n_head))

    loads = [
        pltpu.make_async_copy(source, target, local_sem.at[i])
        for i, (source, target) in enumerate(
            (
                (q_hbm, q_ref),
                (nk_hbm, nk_ref),
                (nv_hbm, nv_ref),
                (stretch_hbm, stretch_ref),
                (order_hbm, order_ref),
                (k_hbm, kbuf.at[pl.ds(0, cache)]),
                (v_hbm, vbuf.at[pl.ds(0, cache)]),
            )
        )
    ]
    for load in loads:
        load.start()

    barrier = pltpu.get_barrier_semaphore()

    def greet(step):
        pl.semaphore_signal(
            barrier, inc=1, device_id=place(lax.rem(me + step, n)), device_id_type=MESH
        )

    each(1, n, greet)

    for load in loads[:3]:
        load.wait()
    block = q_ref[...].astype(F32)
    for h in range(n_head):
        pieces = [
            block[:, (h * heads + i) * HEAD_WIDTH : (h * heads + i + 1) * HEAD_WIDTH]
            for i in range(heads)
        ]
        qsend[h] = jnp.concatenate(pieces, axis=0).astype(BF16)
    blank = jnp.zeros((TILE - rows, width), F32)
    for t, ref in enumerate((nk_ref, nv_ref)):
        new = ref[...].astype(F32)
        for h in range(n_head):
            part = new[:, h * width : (h + 1) * width]
            fresh[h, t] = jnp.concatenate([part, blank], axis=0).astype(BF16)

    pl.semaphore_wait(barrier, n - 1)

    spot = pl.ds(pl.multiple_of(cache + TILE * head, TILE), TILE)
    swaps = []
    for step in range(1, n_head):
        to = lax.rem(head + step, n_head)
        for t, buf in enumerate((kbuf, vbuf)):
            swap = pltpu.make_async_remote_copy(
                src_ref=fresh.at[to, t],
                dst_ref=buf.at[spot],
                send_sem=kv_send.at[step - 1, t],
                recv_sem=kv_recv.at[step - 1, t],
                device_id=(ctx, to),
                device_id_type=MESH,
            )
            swap.start()
            swaps.append(swap)

    def send_queries(step):
        to_ctx, to_head = place(lax.rem(me + n - step, n))
        pltpu.make_async_remote_copy(
            src_ref=qsend.at[to_head],
            dst_ref=qrecv.at[me],
            send_sem=q_sems.at[0],
            recv_sem=q_sems.at[1],
            device_id=(to_ctx, to_head),
            device_id_type=MESH,
        ).start()

    each(1, n, send_queries)
    qrecv[me] = qsend[head]
    kbuf[spot] = fresh[head, 0]
    vbuf[spot] = fresh[head, 1]

    for load in loads[3:]:
        load.wait()

    def start_of(slot):
        return order_ref[slot // per_half] * half + lax.rem(slot, per_half) * rows

    total_keys = cache + TILE * n_head
    split = (cache // 128) * 128
    column = lax.broadcasted_iota(jnp.int32, (1, total_keys), 1)
    key_pos = jnp.where(column + ctx * cache < stretch_ref[0], -1, FAR)
    for h in range(n_head):
        offset = column - (cache + TILE * h)
        pos = jnp.where(offset < rows, start_of(ctx * n_head + h) + offset, FAR)
        key_pos = jnp.where(offset >= 0, pos, key_pos)

    for swap in swaps:
        swap.wait()
    q_all = qrecv.at[pl.ds(0, n - 1)]
    q_done = pltpu.make_async_remote_copy(
        src_ref=q_all,
        dst_ref=q_all,
        send_sem=q_sems.at[0],
        recv_sem=q_sems.at[1],
        device_id=(ctx, head),
        device_id_type=MESH,
    )
    q_done.wait_recv()

    group = min(n, 32)
    size = group * lines
    scale = 1.0 / math.sqrt(HEAD_WIDTH)

    def attend(index):
        first = index * group
        line = lax.broadcasted_iota(jnp.int32, (size, HEAD_WIDTH), 0)
        line = lax.rem(line, lines)
        kv_of = line // (lines // kv_heads)
        q = qrecv[pl.ds(first, group)].astype(F32).reshape(size, HEAD_WIDTH)
        q = jnp.concatenate(
            [jnp.where(kv_of == g, q, 0.0) for g in range(kv_heads)], axis=1
        ).astype(BF16)
        scores = (
            lax.dot_general(
                q, kbuf[...], (((1,), (1,)), ((), ())), preferred_element_type=F32
            )
            * scale
        )
        tail = total_keys - split
        query_pos = jnp.concatenate(
            [jnp.full((lines, tail), start_of(first + i), jnp.int32) for i in range(group)],
            axis=0,
        )
        query_pos = query_pos + lax.rem(
            lax.broadcasted_iota(jnp.int32, (size, tail), 0), rows
        )
        old = jnp.where(key_pos[:, :split] < 0, scores[:, :split], NEG_FILL)
        new = jnp.where(key_pos[:, split:] <= query_pos, scores[:, split:], NEG_FILL)
        scores = jnp.concatenate([old, new], axis=1)
        peak = jnp.max(scores, axis=1, keepdims=True)
        weights = jnp.exp(scores - peak)
        total = jnp.sum(weights, axis=1, keepdims=True)
        sums = lax.dot_general(
            weights.astype(BF16),
            vbuf[...],
            (((1,), (0,)), ((), ())),
            preferred_element_type=F32,
        )
        part = sums[:, :HEAD_WIDTH]
        for g in range(1, kv_heads):
            part = jnp.where(kv_of == g, sums[:, g * HEAD_WIDTH : (g + 1) * HEAD_WIDTH], part)
        part = part / total
        mass = peak + jnp.log(total)
        high = mass.astype(BF16).astype(F32)
        rest = mass - high
        mid = rest.astype(BF16).astype(F32)
        low = rest - mid
        lane = lax.broadcasted_iota(jnp.int32, (size, HEAD_WIDTH), 1)
        stat = jnp.where(lane < lines, high, jnp.where(lane < 2 * lines, mid, low))
        stat = jnp.where((lane < 3 * lines) & (lax.rem(lane, lines) == line), stat, 0.0)
        stat = jnp.sum(stat.reshape(group, lines, HEAD_WIDTH), axis=1, keepdims=True)
        osend[pl.ds(first, group), 0:lines] = part.reshape(group, lines, HEAD_WIDTH).astype(BF16)
        osend[pl.ds(first, group), lines : lines + STAT_ROWS] = jnp.broadcast_to(
            stat, (group, STAT_ROWS, HEAD_WIDTH)
        ).astype(BF16)

    each(0, n // group, attend)

    def send_parts(step):
        slot = lax.rem(me + step, n)
        pltpu.make_async_remote_copy(
            src_ref=osend.at[slot],
            dst_ref=orecv.at[me],
            send_sem=o_sems.at[0],
            recv_sem=o_sems.at[1],
            device_id=place(slot),
            device_id_type=MESH,
        ).start()

    each(1, n, send_parts)
    orecv[me] = osend[me]
    q_done.wait_send()
    o_all = orecv.at[pl.ds(0, n - 1)]
    o_done = pltpu.make_async_remote_copy(
        src_ref=o_all,
        dst_ref=o_all,
        send_sem=o_sems.at[0],
        recv_sem=o_sems.at[1],
        device_id=(ctx, head),
        device_id_type=MESH,
    )
    o_done.wait_recv()

    lane = lax.broadcasted_iota(jnp.int32, (lines, HEAD_WIDTH), 1)
    line = lax.broadcasted_iota(jnp.int32, (lines, HEAD_WIDTH), 0)
    mine = (lane < 3 * lines) & (lax.rem(lane, lines) == line)
    parts = orecv[:, 0:lines].astype(F32).reshape(n_ctx, n_head, lines, HEAD_WIDTH)
    stats = orecv[:, lines : lines + STAT_ROWS].astype(F32)
    stats = stats.reshape(n_ctx, n_head, STAT_ROWS, HEAD_WIDTH)
    for h in range(n_head):
        spread = jnp.where(mine[None], stats[:, h, 0:1], 0.0)
        mass = jnp.sum(spread, axis=2, keepdims=True)
        top = jnp.max(mass, axis=0, keepdims=True)
        share = jnp.exp(mass - top)
        result = jnp.sum(share * parts[:, h], axis=0) / jnp.sum(share, axis=0)
        for i in range(heads):
            at = (h * heads + i) * HEAD_WIDTH
            out_ref[:, at : at + HEAD_WIDTH] = result[i * rows : (i + 1) * rows].astype(BF16)
    o_done.wait_send()


def on_device(
    n_ctx,
    n_head,
    queries,
    new_block_keys,
    new_block_values,
    stored_keys,
    stored_values,
    stretch_start,
    block_order,
):
    n = n_ctx * n_head
    rows = queries.shape[0]
    cache, width = stored_keys.shape
    lines = QUERY_HEADS // n_head * rows
    total_keys = cache + TILE * n_head
    dma = pltpu.SemaphoreType.DMA
    return pl.pallas_call(
        functools.partial(kernel, n_ctx, n_head),
        out_shape=jax.ShapeDtypeStruct(queries.shape, BF16),
        in_specs=[pl.BlockSpec(memory_space=pltpu.HBM)] * 7,
        out_specs=pl.BlockSpec(memory_space=pltpu.VMEM),
        scratch_shapes=[
            pltpu.SMEM(stretch_start.shape, jnp.int32),
            pltpu.SMEM(block_order.shape, jnp.int32),
            pltpu.VMEM(queries.shape, BF16),
            pltpu.VMEM(new_block_keys.shape, BF16),
            pltpu.VMEM(new_block_values.shape, BF16),
            pltpu.VMEM((n_head, lines, HEAD_WIDTH), BF16),
            pltpu.VMEM((n, lines, HEAD_WIDTH), BF16),
            pltpu.VMEM((total_keys, width), BF16),
            pltpu.VMEM((total_keys, width), BF16),
            pltpu.VMEM((n_head, 2, TILE, width), BF16),
            pltpu.VMEM((n, lines + STAT_ROWS, HEAD_WIDTH), BF16),
            pltpu.VMEM((n, lines + STAT_ROWS, HEAD_WIDTH), BF16),
            dma((7,)),
            dma((2,)),
            dma((n_head - 1, 2)),
            dma((n_head - 1, 2)),
            dma((2,)),
        ],
        compiler_params=pltpu.CompilerParams(
            collective_id=0, has_side_effects=True, vmem_limit_bytes=48 * 1024 * 1024
        ),
    )(
        stretch_start,
        *[
            pltpu.with_memory_space_constraint(x, pltpu.HBM)
            for x in (
                block_order,
                queries,
                new_block_keys,
                new_block_values,
                stored_keys,
                stored_values,
            )
        ],
    )


def solution(mesh):
    return jax.shard_map(
        functools.partial(on_device, mesh.shape["ctx"], mesh.shape["head"]),
        mesh=mesh,
        in_specs=(
            P(("ctx", "head"), None),
            P(("ctx", "head"), None),
            P(("ctx", "head"), None),
            P("ctx", "head"),
            P("ctx", "head"),
            P(),
            P(),
        ),
        out_specs=P(("ctx", "head"), None),
        check_vma=False,
    )
```

```python
import functools
import math

import jax
import jax.numpy as jnp
from jax import lax
from jax.experimental import pallas as pl
from jax.experimental.pallas import tpu as pltpu
from jax.sharding import PartitionSpec as P

QUERY_HEADS = 16
KEY_VALUE_HEADS = 4
HEAD_WIDTH = 128
NEG_FILL = -1e30
FAR = 2**30
TILE = 16
STAT_ROWS = 2
MESH = pl.DeviceIdType.MESH
F32 = jnp.float32
BF16 = jnp.bfloat16


def each(first, count, body):
    if count - first <= 64:
        for step in range(first, count):
            body(step)
    else:
        lax.fori_loop(first, count, lambda step, _: body(step), None)


def kernel(
    n_ctx,
    n_head,
    stretch_hbm,
    order_hbm,
    q_hbm,
    nk_hbm,
    nv_hbm,
    k_hbm,
    v_hbm,
    out_ref,
    stretch_ref,
    order_ref,
    q_ref,
    nk_ref,
    nv_ref,
    qsend,
    qrecv,
    kbuf,
    vbuf,
    fresh,
    osend,
    orecv,
    local_sem,
    q_sems,
    kv_send,
    kv_recv,
    o_sems,
):
    n = n_ctx * n_head
    rows = q_hbm.shape[0]
    cache = k_hbm.shape[0]
    width = k_hbm.shape[1]
    kv_heads = width // HEAD_WIDTH
    heads = QUERY_HEADS // n_head
    lines = heads * rows
    half = rows * n_head // 2
    per_half = half // rows
    ctx = lax.axis_index("ctx")
    head = lax.axis_index("head")
    me = ctx * n_head + head

    def place(slot):
        return (slot // n_head, lax.rem(slot, n_head))

    loads = [
        pltpu.make_async_copy(source, target, local_sem.at[i])
        for i, (source, target) in enumerate(
            (
                (q_hbm, q_ref),
                (nk_hbm, nk_ref),
                (nv_hbm, nv_ref),
                (stretch_hbm, stretch_ref),
                (order_hbm, order_ref),
                (k_hbm, kbuf.at[pl.ds(0, cache)]),
                (v_hbm, vbuf.at[pl.ds(0, cache)]),
            )
        )
    ]
    for load in loads:
        load.start()

    barrier = pltpu.get_barrier_semaphore()

    def greet(step):
        pl.semaphore_signal(
            barrier, inc=1, device_id=place(lax.rem(me + step, n)), device_id_type=MESH
        )

    each(1, n, greet)

    for load in loads[:3]:
        load.wait()
    block = q_ref[...].astype(F32)
    for h in range(n_head):
        pieces = [
            block[:, (h * heads + i) * HEAD_WIDTH : (h * heads + i + 1) * HEAD_WIDTH]
            for i in range(heads)
        ]
        qsend[h] = jnp.concatenate(pieces, axis=0).astype(BF16)
    blank = jnp.zeros((TILE - rows, width), F32)
    for t, ref in enumerate((nk_ref, nv_ref)):
        new = ref[...].astype(F32)
        for h in range(n_head):
            part = new[:, h * width : (h + 1) * width]
            fresh[h, t] = jnp.concatenate([part, blank], axis=0).astype(BF16)

    pl.semaphore_wait(barrier, n - 1)

    spot = pl.ds(pl.multiple_of(cache + TILE * head, TILE), TILE)
    swaps = []
    for step in range(1, n_head):
        to = lax.rem(head + step, n_head)
        for t, buf in enumerate((kbuf, vbuf)):
            swap = pltpu.make_async_remote_copy(
                src_ref=fresh.at[to, t],
                dst_ref=buf.at[spot],
                send_sem=kv_send.at[step - 1, t],
                recv_sem=kv_recv.at[step - 1, t],
                device_id=(ctx, to),
                device_id_type=MESH,
            )
            swap.start()
            swaps.append(swap)

    def send_queries(step):
        to_ctx, to_head = place(lax.rem(me + n - step, n))
        pltpu.make_async_remote_copy(
            src_ref=qsend.at[to_head],
            dst_ref=qrecv.at[me],
            send_sem=q_sems.at[0],
            recv_sem=q_sems.at[1],
            device_id=(to_ctx, to_head),
            device_id_type=MESH,
        ).start()

    each(1, n, send_queries)
    qrecv[me] = qsend[head]
    kbuf[spot] = fresh[head, 0]
    vbuf[spot] = fresh[head, 1]

    for load in loads[3:]:
        load.wait()

    def start_of(slot):
        return order_ref[slot // per_half] * half + lax.rem(slot, per_half) * rows

    total_keys = cache + TILE * n_head
    split = (cache // 128) * 128
    column = lax.broadcasted_iota(jnp.int32, (1, total_keys), 1)
    key_pos = jnp.where(column + ctx * cache < stretch_ref[0], -1, FAR)
    for h in range(n_head):
        offset = column - (cache + TILE * h)
        pos = jnp.where(offset < rows, start_of(ctx * n_head + h) + offset, FAR)
        key_pos = jnp.where(offset >= 0, pos, key_pos)

    for swap in swaps:
        swap.wait()
    q_all = qrecv.at[pl.ds(0, n - 1)]
    q_done = pltpu.make_async_remote_copy(
        src_ref=q_all,
        dst_ref=q_all,
        send_sem=q_sems.at[0],
        recv_sem=q_sems.at[1],
        device_id=(ctx, head),
        device_id_type=MESH,
    )
    q_done.wait_recv()

    group = n // 2 if n <= 64 else 32
    groups = n // group
    size = group * lines
    scale = 1.0 / math.sqrt(HEAD_WIDTH)

    def attend(index):
        first = lax.rem(me // group + index, groups) * group
        line = lax.broadcasted_iota(jnp.int32, (size, HEAD_WIDTH), 0)
        line = lax.rem(line, lines)
        kv_of = line // (lines // kv_heads)
        q = qrecv[pl.ds(first, group)].astype(F32).reshape(size, HEAD_WIDTH)
        q = jnp.concatenate(
            [jnp.where(kv_of == g, q, 0.0) for g in range(kv_heads)], axis=1
        ).astype(BF16)
        scores = (
            lax.dot_general(
                q, kbuf[...], (((1,), (1,)), ((), ())), preferred_element_type=F32
            )
            * scale
        )
        tail = total_keys - split
        query_pos = jnp.concatenate(
            [jnp.full((lines, tail), start_of(first + i), jnp.int32) for i in range(group)],
            axis=0,
        )
        query_pos = query_pos + lax.rem(
            lax.broadcasted_iota(jnp.int32, (size, tail), 0), rows
        )
        old = jnp.where(key_pos[:, :split] < 0, scores[:, :split], NEG_FILL)
        new = jnp.where(key_pos[:, split:] <= query_pos, scores[:, split:], NEG_FILL)
        scores = jnp.concatenate([old, new], axis=1)
        peak = jnp.max(scores, axis=1, keepdims=True)
        weights = jnp.exp(scores - peak)
        total = jnp.sum(weights, axis=1, keepdims=True)
        sums = lax.dot_general(
            weights.astype(BF16),
            vbuf[...],
            (((1,), (0,)), ((), ())),
            preferred_element_type=F32,
        )
        part = sums[:, :HEAD_WIDTH]
        for g in range(1, kv_heads):
            part = jnp.where(kv_of == g, sums[:, g * HEAD_WIDTH : (g + 1) * HEAD_WIDTH], part)
        part = part / total
        mass = peak + jnp.log(total)
        high = mass.astype(BF16).astype(F32)
        rest = mass - high
        mid = rest.astype(BF16).astype(F32)
        low = rest - mid
        lane = lax.broadcasted_iota(jnp.int32, (size, HEAD_WIDTH), 1)
        stat = jnp.where(lane < lines, high, jnp.where(lane < 2 * lines, mid, low))
        stat = jnp.where((lane < 3 * lines) & (lax.rem(lane, lines) == line), stat, 0.0)
        stat = jnp.sum(stat.reshape(group, lines, HEAD_WIDTH), axis=1, keepdims=True)
        osend[pl.ds(first, group), 0:lines] = part.reshape(group, lines, HEAD_WIDTH).astype(BF16)
        osend[pl.ds(first, group), lines : lines + STAT_ROWS] = jnp.broadcast_to(
            stat, (group, STAT_ROWS, HEAD_WIDTH)
        ).astype(BF16)


        own = isinstance(index, int) and index == 0

        def send_part(step):
            slot = first + lax.rem(me + step, group)
            pltpu.make_async_remote_copy(
                src_ref=osend.at[slot],
                dst_ref=orecv.at[me],
                send_sem=o_sems.at[0],
                recv_sem=o_sems.at[1],
                device_id=place(slot),
                device_id_type=MESH,
            ).start()

        each(1 if own else 0, group, send_part)

    attend(0)
    each(1, groups, attend)
    orecv[me] = osend[me]
    q_done.wait_send()
    o_all = orecv.at[pl.ds(0, n - 1)]
    o_done = pltpu.make_async_remote_copy(
        src_ref=o_all,
        dst_ref=o_all,
        send_sem=o_sems.at[0],
        recv_sem=o_sems.at[1],
        device_id=(ctx, head),
        device_id_type=MESH,
    )
    o_done.wait_recv()

    lane = lax.broadcasted_iota(jnp.int32, (lines, HEAD_WIDTH), 1)
    line = lax.broadcasted_iota(jnp.int32, (lines, HEAD_WIDTH), 0)
    mine = (lane < 3 * lines) & (lax.rem(lane, lines) == line)
    parts = orecv[:, 0:lines].astype(F32).reshape(n_ctx, n_head, lines, HEAD_WIDTH)
    stats = orecv[:, lines : lines + STAT_ROWS].astype(F32)
    stats = stats.reshape(n_ctx, n_head, STAT_ROWS, HEAD_WIDTH)
    for h in range(n_head):
        spread = jnp.where(mine[None], stats[:, h, 0:1], 0.0)
        mass = jnp.sum(spread, axis=2, keepdims=True)
        top = jnp.max(mass, axis=0, keepdims=True)
        share = jnp.exp(mass - top)
        result = jnp.sum(share * parts[:, h], axis=0) / jnp.sum(share, axis=0)
        for i in range(heads):
            at = (h * heads + i) * HEAD_WIDTH
            out_ref[:, at : at + HEAD_WIDTH] = result[i * rows : (i + 1) * rows].astype(BF16)
    o_done.wait_send()


def on_device(
    n_ctx,
    n_head,
    queries,
    new_block_keys,
    new_block_values,
    stored_keys,
    stored_values,
    stretch_start,
    block_order,
):
    n = n_ctx * n_head
    rows = queries.shape[0]
    cache, width = stored_keys.shape
    lines = QUERY_HEADS // n_head * rows
    total_keys = cache + TILE * n_head
    dma = pltpu.SemaphoreType.DMA
    return pl.pallas_call(
        functools.partial(kernel, n_ctx, n_head),
        out_shape=jax.ShapeDtypeStruct(queries.shape, BF16),
        in_specs=[pl.BlockSpec(memory_space=pltpu.HBM)] * 7,
        out_specs=pl.BlockSpec(memory_space=pltpu.VMEM),
        scratch_shapes=[
            pltpu.SMEM(stretch_start.shape, jnp.int32),
            pltpu.SMEM(block_order.shape, jnp.int32),
            pltpu.VMEM(queries.shape, BF16),
            pltpu.VMEM(new_block_keys.shape, BF16),
            pltpu.VMEM(new_block_values.shape, BF16),
            pltpu.VMEM((n_head, lines, HEAD_WIDTH), BF16),
            pltpu.VMEM((n, lines, HEAD_WIDTH), BF16),
            pltpu.VMEM((total_keys, width), BF16),
            pltpu.VMEM((total_keys, width), BF16),
            pltpu.VMEM((n_head, 2, TILE, width), BF16),
            pltpu.VMEM((n, lines + STAT_ROWS, HEAD_WIDTH), BF16),
            pltpu.VMEM((n, lines + STAT_ROWS, HEAD_WIDTH), BF16),
            dma((7,)),
            dma((2,)),
            dma((n_head - 1, 2)),
            dma((n_head - 1, 2)),
            dma((2,)),
        ],
        compiler_params=pltpu.CompilerParams(
            collective_id=0, has_side_effects=True, vmem_limit_bytes=48 * 1024 * 1024
        ),
    )(
        stretch_start,
        *[
            pltpu.with_memory_space_constraint(x, pltpu.HBM)
            for x in (
                block_order,
                queries,
                new_block_keys,
                new_block_values,
                stored_keys,
                stored_values,
            )
        ],
    )


def solution(mesh):
    return jax.shard_map(
        functools.partial(on_device, mesh.shape["ctx"], mesh.shape["head"]),
        mesh=mesh,
        in_specs=(
            P(("ctx", "head"), None),
            P(("ctx", "head"), None),
            P(("ctx", "head"), None),
            P("ctx", "head"),
            P("ctx", "head"),
            P(),
            P(),
        ),
        out_specs=P(("ctx", "head"), None),
        check_vma=False,
    )
```
